256 devices in a mesh: ew: 8 (over y, z_hi), ns: 32 (over z_lo, x, core).
Axes of the slice: x: 4, y: 4, z: 8 (z_hi: 2, z_lo: 4; z = z_hi * 4 + z_lo), core: 2. Of those that a mesh axis runs over, the one named last changes fastest.
Arguments:
- couplings: bfloat16 [8, 32, 16, 128, 2048], P('ew', 'ns'), may hold values from -0.125 to 0.125
- inverses: bfloat16 [8, 32, 16, 128, 128], P('ew', 'ns'), as said below
- pattern: int32 [8, 32, 16, 16], P('ew', 'ns'), may hold values 0 or 1
- counts: int32 [8, 32], P('ew', 'ns'), may hold values from 1 to 16, as said below
- basis: bfloat16 [8, 32, 128, 2048], P('ew', 'ns'), may hold values from -0.125 to 0.125
Outputs:
- south_front: float32 [8, 32, 768, 768], P('ew', 'ns')
- west_front: float32 [8, 32, 256, 256], P('ew', 'ns')
- coarse: float32 [8, 32, 128, 128], P('ew', 'ns')
The draws below stay inside these ranges and needn't reach their ends.
Inputs may be any that keep to these rules, and one draw needn't show every extreme that they name: `counts`: some subdomain has exactly 16 live block columns. `inverses`: each block is symmetric.
All inputs are finite; a program needn't handle non-finite values. No bound on the sum of `pattern` on one device may be relied on, other than what follows from the above.
Results may differ from the reference program's by a relative error of at most 0.0015.
Values may be sent and summed in bfloat16 or wider, within the bound.
No kernel may reach another device: no remote copies, remote signals or barrier semaphores. Data moves between devices by JAX's collectives and lax.ppermute only.
A program may use at most 128 MiB of HBM per device.

```python
import jax
import jax.numpy as jnp
from jax import lax

B = 128
SN = 6
SE = 2
R = 128
K = 16
N_EW = 8
N_NS = 32


def draw_inverses(key, part):
    first, second = jax.random.split(jax.random.fold_in(key, 11))
    shape = (N_EW, N_NS, K, B, B)
    noise = jax.random.normal(first, shape, jnp.float32)
    symmetric = (noise + jnp.swapaxes(noise, -1, -2)) * (0.5 / jnp.sqrt(2.0 * B))
    diagonal = jax.random.uniform(second, shape[:-1], jnp.float32, 1.5, 3.0)
    identity = jnp.eye(B, dtype=jnp.float32)
    return (symmetric * (1.0 - identity) + diagonal[..., None] * identity).astype(jnp.bfloat16)


def draw_counts(key, part):
    first, second = jax.random.split(jax.random.fold_in(key, 23))
    base = jax.random.randint(first, (N_EW, N_NS), 1, K + 1)
    picked = jax.random.randint(second, (), 0, N_EW * N_NS)
    places = jnp.arange(N_EW * N_NS, dtype=jnp.int32).reshape(N_EW, N_NS)
    return jnp.where(places == picked, K, base).astype(jnp.int32)


def plant(drawn, stream_key, smallest, high):
    longest = drawn.shape.index(max(drawn.shape))
    spots = []
    for shift in (0, 1):
        where = [jax.random.randint(jax.random.fold_in(stream_key, axis), (), 0, length) for axis, length in enumerate(drawn.shape)]
        where[longest] = (where[longest] + shift) % drawn.shape[longest]
        spots.append(tuple(where))
    return drawn.at[spots[0]].set(smallest).at[spots[1]].set(high)


def level_of(stream_key, shape, pieces, smallest, largest):
    loudness = 1.0
    for dim, shards_of in pieces:
        steps = jax.random.uniform(jax.random.fold_in(jax.random.fold_in(stream_key, 6), dim), (shards_of,), jnp.float32, smallest / len(pieces), largest / len(pieces))
        loudness = loudness * jnp.repeat(jnp.exp(steps), shape[dim] // shards_of).reshape((-1,) + (1,) * (len(shape) - 1 - dim))
    return loudness


def normal_values(own_key, shape, deviation, reach, shards=(), kind=jnp.bfloat16):
    array = jax.random.normal(own_key, shape, jnp.float32) * deviation
    if len(shards) > 0:
        array = level_of(own_key, shape, shards, -0.22, 0.18) * array
    return jnp.clip(array, min=-reach, max=reach).astype(kind)


def setup_inputs(seed: int = 0) -> dict:
    key_list = jax.random.split(jax.random.key(seed), 6)
    return {
        "couplings": normal_values(key_list[0], (N_EW, N_NS, K, B, (2 * SN + 2 * SE) * B), (K * B) ** -0.5, 0.125, ((0, 8), (1, 32))),
        "inverses": draw_inverses(jax.random.fold_in(key_list[5], 71), 0),
        "pattern": plant((jax.random.randint(key_list[2], (N_EW, N_NS, K, 2 * SN + 2 * SE), 0, 4) < 3).astype(jnp.int32), jax.random.fold_in(key_list[2], 1), 0, 1),
        "counts": draw_counts(jax.random.fold_in(key_list[5], 71), 0),
        "basis": normal_values(key_list[4], (N_EW, N_NS, R, N_EW * SE * B), (N_EW * SE * B) ** -0.5, 0.125, ((0, 8), (1, 32))),
    }


def edge_update(slab, inverse):
    solved = jnp.einsum('kab,kbc->kac', inverse.astype(jnp.float32), slab.astype(jnp.float32)).astype(jnp.bfloat16)
    return -jnp.einsum('kbi,kbj->ij', slab.astype(jnp.float32), solved.astype(jnp.float32))


def device_updates(items):
    coupling, inverse, touched, count = items
    columns = jnp.repeat(touched, B, axis=1)
    live = (jnp.arange(K, dtype=jnp.int32) < count).astype(jnp.int32)[:, None]
    keep = (columns * live).astype(jnp.bfloat16)
    masked = coupling * keep[:, None, :]
    north_start = SN * B
    west_start = 2 * SN * B
    east_start = west_start + SE * B
    south_part = edge_update(masked[:, :, 0:north_start], inverse)
    north_part = edge_update(masked[:, :, north_start:west_start], inverse)
    west_part = edge_update(masked[:, :, west_start:east_start], inverse)
    east_part = edge_update(masked[:, :, east_start:east_start + SE * B], inverse)
    return south_part, north_part, west_part, east_part


def reference(couplings, inverses, pattern, counts, basis):
    width = (2 * SN + 2 * SE) * B
    flat = (couplings.reshape(N_EW * N_NS, K, B, width), inverses.reshape(N_EW * N_NS, K, B, B),
            pattern.reshape(N_EW * N_NS, K, 2 * SN + 2 * SE), counts.reshape(N_EW * N_NS))
    south_part, north_part, west_part, east_part = lax.map(device_updates, flat)
    south_part = south_part.reshape(N_EW, N_NS, SN * B, SN * B)
    north_part = north_part.reshape(N_EW, N_NS, SN * B, SN * B)
    west_part = west_part.reshape(N_EW, N_NS, SE * B, SE * B)
    east_part = east_part.reshape(N_EW, N_NS, SE * B, SE * B)
    from_south = jnp.concatenate([jnp.zeros_like(north_part[:, :1]), north_part[:, :-1]], axis=1)
    south_front = south_part + from_south
    from_west = jnp.concatenate([jnp.zeros_like(east_part[:1]), east_part[:-1]], axis=0)
    west_front = west_part + from_west
    front_half = west_front.astype(jnp.bfloat16)
    blocks = basis.reshape(N_EW, N_NS, R, N_EW, SE * B).astype(jnp.float32)
    projected = jnp.einsum('enrjk,jnkl->enrjl', blocks, front_half.astype(jnp.float32)).astype(jnp.bfloat16)
    coarse = jnp.einsum('enrjl,ensjl->enrs', projected.astype(jnp.float32), blocks)
    return south_front, west_front, coarse
```

```python
import functools

import jax
import jax.numpy as jnp
from jax import lax
from jax.experimental import pallas as pl
from jax.experimental.pallas import tpu as pltpu
from jax.sharding import PartitionSpec as P

B = 128
SN = 6
SE = 2
NS_W = SN * B
EW_W = SE * B
CHUNK = 4


def edges_kernel(first_block, edge, keep_ref, x_ref, inv_ref, *rest):
    outs, (m_ref, s_ref) = rest[:-2], rest[-2:]
    step = pl.program_id(0)
    width = x_ref.shape[-1]
    for kk in range(CHUNK):
        rows = slice(kk * B, (kk + 1) * B)
        for j in range(width // B):
            cols = slice(j * B, (j + 1) * B)
            keep = keep_ref[step * CHUNK + kk, first_block + j].astype(jnp.float32).astype(jnp.bfloat16)
            m_ref[rows, cols] = x_ref[0, 0, kk, :, cols] * keep
        solved = jnp.dot(inv_ref[0, 0, kk], m_ref[rows, :], preferred_element_type=jnp.float32)
        s_ref[rows, :] = solved.astype(jnp.bfloat16)
    for index, out in enumerate(outs):
        cols = slice(index * edge, (index + 1) * edge)
        part = lax.dot_general(
            m_ref[:, cols], s_ref[:, cols], (((0,), (0,)), ((), ())), preferred_element_type=jnp.float32
        )

        @pl.when(step == 0)
        def _():
            out[...] = -part

        @pl.when(step > 0)
        def _():
            out[...] = out[...] - part


def edges(name, coupling, inverse, keep, start, edge, count):
    blocks = coupling.shape[2]
    width = edge * count
    return pl.pallas_call(
        functools.partial(edges_kernel, start // B, edge),
        out_shape=[jax.ShapeDtypeStruct((edge, edge), jnp.float32)] * count,
        grid_spec=pltpu.PrefetchScalarGridSpec(
            num_scalar_prefetch=1,
            grid=(blocks // CHUNK,),
            in_specs=[
                pl.BlockSpec((1, 1, CHUNK, B, width), lambda c, keep: (0, 0, c, 0, start // width)),
                pl.BlockSpec((1, 1, CHUNK, B, B), lambda c, keep: (0, 0, c, 0, 0)),
            ],
            out_specs=[pl.BlockSpec((edge, edge), lambda c, keep: (0, 0))] * count,
            scratch_shapes=[
                pltpu.VMEM((CHUNK * B, width), jnp.bfloat16),
                pltpu.VMEM((CHUNK * B, width), jnp.bfloat16),
            ],
        ),
        cost_estimate=pl.CostEstimate(
            flops=2 * blocks * B * (B * width + edge * edge * count),
            transcendentals=0,
            bytes_accessed=2 * blocks * B * (width + B) + 4 * edge * edge * count,
        ),
        name=name,
    )(keep, coupling, inverse)


def from_behind(block, axis, distance):
    devices = range(lax.axis_size(axis))
    route = [(i - distance, i) for i in devices if i - distance in devices]
    return lax.ppermute(block, axis, route)


def ring(block, axis, distance):
    size = lax.axis_size(axis)
    return lax.ppermute(block, axis, [(i, (i + distance) % size) for i in range(size)])


def coarse_kernel(me_ref, q_ref, *refs):
    fronts, out_ref = refs[:-1], refs[-1]
    size = len(fronts)
    total = jnp.zeros(out_ref.shape, jnp.float32)
    for i in range(size):
        owner = lax.rem(me_ref[0] + size - 2 * (i // 2), size)
        if i % 2:
            owner = owner + 1 - 2 * lax.rem(owner, 2)
        q = q_ref[0, 0, :, pl.ds(pl.multiple_of(owner * EW_W, EW_W), EW_W)]
        projected = jnp.dot(q, fronts[i][...], preferred_element_type=jnp.float32).astype(jnp.bfloat16)
        total = total + lax.dot_general(
            projected, q, (((1,), (1,)), ((), ())), preferred_element_type=jnp.float32
        )
    out_ref[...] = total


def coarse_of(me, basis, fronts):
    rank = basis.shape[2]
    vmem = pl.BlockSpec(memory_space=pltpu.VMEM)
    return pl.pallas_call(
        coarse_kernel,
        out_shape=jax.ShapeDtypeStruct((rank, rank), jnp.float32),
        in_specs=[pl.BlockSpec(memory_space=pltpu.SMEM)] + [vmem] * (1 + len(fronts)),
        out_specs=vmem,
        name="coarse",
    )(me, basis, *fronts)


def shards(couplings, inverses, pattern, counts, basis):
    touched = pattern[0, 0]
    blocks = touched.shape[0]
    live = (jnp.arange(blocks, dtype=jnp.int32) < counts[0, 0]).astype(jnp.int32)[:, None]
    keep = touched * live
    west_start = 2 * NS_W
    west, east = edges("east_west", couplings, inverses, keep, west_start, EW_W, 2)
    with jax.named_scope("shift_east"):
        from_west = from_behind(east, "ew", 1)
    (north,) = edges("north", couplings, inverses, keep, NS_W, NS_W, 1)
    with jax.named_scope("shift_north"):
        from_south = from_behind(north, "ns", 1)
    west_front = west + from_west
    half = west_front.astype(jnp.bfloat16)
    size = lax.axis_size("ew")
    with jax.named_scope("across"):
        other = lax.ppermute(half, "ew", [(i, i ^ 1) for i in range(size)])
    with jax.named_scope("row_own"):
        own_row = [ring(half, "ew", d) for d in range(2, size, 2)]
    (south,) = edges("south", couplings, inverses, keep, 0, NS_W, 1)
    with jax.named_scope("row_other"):
        other_row = [ring(other, "ew", d) for d in range(2, size, 2)]
    fronts = []
    for pair in zip([half] + own_row, [other] + other_row):
        fronts.extend(pair)
    me = lax.axis_index("ew").astype(jnp.int32).reshape(1)
    coarse = coarse_of(me, basis, fronts)
    south_front = south + from_south
    return (south_front[None, None], west_front[None, None], coarse[None, None])


def solution(mesh):
    return jax.shard_map(
        shards,
        mesh=mesh,
        in_specs=(
            P("ew", "ns", None, None, None),
            P("ew", "ns", None, None, None),
            P("ew", "ns", None, None),
            P("ew", "ns"),
            P("ew", "ns", None, None),
        ),
        out_specs=(P("ew", "ns", None, None), P("ew", "ns", None, None), P("ew", "ns", None, None)),
        check_vma=False,
    )
```
